32 devices in a mesh: pb: 2 (over x), row: 16 (over z, y, core).
Axes of the slice: x: 2, y: 2, z: 4, core: 2. Of those that a mesh axis runs over, the one named last changes fastest.
Arguments:
- force_constants: float32 [9, 4608, 4608], P(None, 'row', 'pb'), may hold values from -0.1 to 3.6, as said below
- offsets: int32 [9, 3], replicated, may hold values from -2 to 2, as said below
- qpoints: int32 [2, 3], replicated, may hold values from 0 to 7
- lower_bound: float32 [2], P('pb'), may hold values from 1.5 to 2.5
- upper_bound: float32 [2], P('pb'), may hold values from 5.5 to 6.5
- start_vectors: float32 [4608, 128], P('row'), may hold values from -6 to 6
Outputs:
- basis: float32 [2, 4608, 128], P('pb', 'row')
- ritz: float32 [2, 64, 128], P('pb')
The draws below stay inside these ranges and needn't reach their ends.
Inputs may be any that keep to these rules, and one draw needn't show every extreme that they name: `force_constants`: cell 0 is symmetric; for 1 <= c <= 4, cell c + 4 is the transpose of cell c, so every D(q) is Hermitian. `offsets`: row 0 is zero; for 1 <= c <= 4, row c + 4 is the negative of row c.
All inputs are finite; a program needn't handle non-finite values.
Results may differ from the reference program's by a relative error of at most 0.00025.
Values sent between devices are 32-bit elements; how exact they have to be, the bound alone decides.
A program may use at most 128 MiB of HBM per device.

```python
import math
import jax
import jax.numpy as jnp
from jax import lax

MODES = 4608
VECTORS = 64
PAIRS = 4
DEG = 2
QDEN = 8
QPTS = 2


def draw_force_constants(key, part):
    sigma = 0.2 / math.sqrt(MODES)
    noise_key = jax.random.fold_in(key, 11)
    diag_key = jax.random.fold_in(key, 13)
    base = jnp.clip(jax.random.normal(noise_key, (PAIRS + 1, MODES, MODES), jnp.float32), -6.0, 6.0) * sigma
    diagonal = jax.random.uniform(diag_key, (MODES,), jnp.float32, 1.5, 3.5)
    home_cell = 0.5 * (base[0] + base[0].T) + jnp.diag(diagonal)
    return jnp.concatenate([home_cell[None], base[1:], jnp.transpose(base[1:], (0, 2, 1))], axis=0)


def draw_offsets(key, part):
    paired = jax.random.randint(jax.random.fold_in(key, 17), (PAIRS, 3), -2, 3, jnp.int32)
    return jnp.concatenate([jnp.zeros((1, 3), jnp.int32), paired, -paired], axis=0)


def with_ends(values, key, smallest, largest):
    shape = values.shape
    index_at = [jax.random.randint(jax.random.fold_in(key, axis), (), 0, shape[axis]) for axis in range(len(shape))]
    values = values.at[tuple(index_at)].set(smallest)
    longest = shape.index(max(shape))
    index_at[longest] = (index_at[longest] + 1) % shape[longest]
    return values.at[tuple(index_at)].set(largest)


def shard_levels(stream_key, dims, shards, low, largest):
    level, own = 1.0, jax.random.fold_in(stream_key, 6)
    for axis_at, blocks in shards:
        heights = jnp.exp(jax.random.uniform(jax.random.fold_in(own, axis_at), (blocks,), jnp.float32, low / len(shards), largest / len(shards)))
        level = level * jnp.repeat(heights, dims[axis_at] // blocks).reshape([-1 if axis == axis_at else 1 for axis in range(len(dims))])
    return level


def normal_values(key, shape, deviation, reach, split=(), kind=jnp.bfloat16):
    values = jax.random.normal(key, shape, jnp.float32) * deviation
    if len(split) > 0:
        values = shard_levels(key, shape, split, -0.22, 0.18) * values
    return jnp.clip(values, min=-reach, max=reach).astype(kind)


def setup_inputs(seed: int = 0) -> dict:
    splits = jax.random.split(jax.random.key(seed), 7)
    force_constants = draw_force_constants(jax.random.fold_in(splits[6], 71), 0)
    offsets = draw_offsets(jax.random.fold_in(splits[6], 71), 0)
    qpoints = with_ends(jax.random.randint(splits[2], (QPTS, 3), 0, QDEN), jax.random.fold_in(splits[2], 1), 0, QDEN - 1).astype(jnp.int32)
    lower_bound = jnp.clip(1.5 + 1.0 * jax.random.uniform(splits[3], (QPTS,), jnp.float32) ** shard_levels(splits[3], (QPTS,), ((0, 2),), -0.2, 0.2), 1.5, 2.5)
    upper_bound = jnp.clip(5.5 + 1.0 * jax.random.uniform(splits[4], (QPTS,), jnp.float32) ** shard_levels(splits[4], (QPTS,), ((0, 2),), -0.2, 0.2), 5.5, 6.5)
    start_vectors = normal_values(splits[5], (MODES, 2 * VECTORS), 1.0, 6.0, ((0, 16),), jnp.float32)
    return dict(force_constants=force_constants, offsets=offsets, qpoints=qpoints, lower_bound=lower_bound, upper_bound=upper_bound, start_vectors=start_vectors)


highest = lax.Precision.HIGHEST

def product(left, right):
    return jnp.dot(left.astype(jnp.float32), right.astype(jnp.float32), precision=highest, preferred_element_type=jnp.float32)

def inner_product(left, right):
    return lax.dot_general(left.astype(jnp.float32), right.astype(jnp.float32), (((0,), (0,)), ((), ())), precision=highest, preferred_element_type=jnp.float32)

def complex_times(left_real, left_imag, right_real, right_imag):
    return (product(left_real, right_real) - product(left_imag, right_imag), product(left_real, right_imag) + product(left_imag, right_real))

def phase_table(qpoints, offsets):
    turns = lax.optimization_barrier(jnp.sum(qpoints[:, None, :] * offsets[None, :, :], axis=2))
    turns = jnp.mod(turns, QDEN)
    angle = 2.0 * math.pi / QDEN * turns.astype(jnp.float32)
    return jnp.stack([jnp.cos(angle), jnp.sin(angle)], axis=1)

def factor_inverse(gram_real, gram_imag):
    order_size = gram_real.shape[0]
    embedded = jnp.stack([jnp.stack([gram_real, -gram_imag], axis=2), jnp.stack([gram_imag, gram_real], axis=2)], axis=1).reshape(2 * order_size, 2 * order_size)
    lower_factor = jnp.linalg.cholesky(embedded)
    identity = jnp.eye(2 * order_size, dtype=gram_real.dtype)
    inverse = jax.scipy.linalg.solve_triangular(lower_factor, identity, lower=True)
    blocks = inverse.reshape(order_size, 2, order_size, 2)
    return (blocks[:, 0, :, 0], blocks[:, 1, :, 0])

def right_block(inverse_real, inverse_imag):
    upper_half = jnp.concatenate([inverse_real.T, -inverse_imag.T], axis=1)
    lower_half = jnp.concatenate([inverse_imag.T, inverse_real.T], axis=1)
    return jnp.concatenate([upper_half, lower_half], axis=0)

def split_gram(matrix, vector_count):
    return (matrix[:vector_count, :vector_count] + matrix[vector_count:, vector_count:], matrix[:vector_count, vector_count:] - matrix[vector_count:, :vector_count])

def chebyshev(vectors, apply_matrix, lower_value, upper_value):
    centre = 0.5 * (upper_value + lower_value)
    spread = 0.5 * (upper_value - lower_value)
    previous = vectors
    current = (apply_matrix(vectors) - centre * vectors) / spread
    for repeat in range(DEG - 1):
        following = 2.0 * (apply_matrix(current) - centre * current) / spread - previous
        previous, current = (current, following)
    return current

def reference(force_constants, offsets, qpoints, lower_bound, upper_bound, start_vectors):
    cell_count = force_constants.shape[0]
    vector_count = start_vectors.shape[1] // 2
    coefficients = phase_table(qpoints, offsets)
    flat_constants = force_constants.reshape(cell_count, MODES * MODES)

    def one_point(point):
        dynamic = product(coefficients[point], flat_constants).reshape(2, MODES, MODES)
        dyn_real = dynamic[0]
        dyn_imag = dynamic[1]

        def apply_matrix(vectors):
            part_real = product(dyn_real, vectors)
            part_imag = product(dyn_imag, vectors)
            return jnp.concatenate([part_real[:, :vector_count] - part_imag[:, vector_count:], part_real[:, vector_count:] + part_imag[:, :vector_count]], axis=1)
        lower_value = lower_bound[point]
        upper_value = upper_bound[point]
        first_pass = chebyshev(start_vectors, apply_matrix, lower_value, upper_value)
        final_pass = chebyshev(first_pass, apply_matrix, lower_value, upper_value)
        image = apply_matrix(final_pass)
        over_real, over_imag = split_gram(inner_product(final_pass, final_pass), vector_count)
        proj_real, proj_imag = split_gram(inner_product(final_pass, image), vector_count)
        inverse_real, inverse_imag = factor_inverse(over_real, over_imag)
        basis_point = math.sqrt(MODES) * product(final_pass, right_block(inverse_real, inverse_imag))
        temp_real, temp_imag = complex_times(proj_real, proj_imag, inverse_real.T, -inverse_imag.T)
        ritz_real, ritz_imag = complex_times(inverse_real, inverse_imag, temp_real, temp_imag)
        return (basis_point, jnp.concatenate([ritz_real, ritz_imag], axis=1))
    basis, ritz = lax.map(one_point, jnp.arange(QPTS, dtype=jnp.int32))
    return (basis, ritz)
```

```python
import functools
import math

import jax
import jax.numpy as jnp
from jax import lax
from jax.experimental import pallas as pl
from jax.experimental.pallas import tpu as pltpu
from jax.sharding import PartitionSpec as P

MODES = 4608
QDEN = 8


highest = lax.Precision.HIGHEST


def product(left, right):
    return jnp.dot(left, right, precision=highest, preferred_element_type=jnp.float32)


def inner_product(left, right):
    return lax.dot_general(
        left, right, (((0,), (0,)), ((), ())), precision=highest, preferred_element_type=jnp.float32
    )


def complex_times(left_real, left_imag, right_real, right_imag):
    return (
        product(left_real, right_real) - product(left_imag, right_imag),
        product(left_real, right_imag) + product(left_imag, right_real),
    )


def phase_table(qpoints, offsets):
    turns = jnp.sum(qpoints[:, None, :] * offsets[None, :, :], axis=2)
    turns = jnp.mod(turns, QDEN)
    angle = 2.0 * math.pi / QDEN * turns.astype(jnp.float32)
    return jnp.stack([jnp.cos(angle), jnp.sin(angle)], axis=1)


def factor_inverse(gram_real, gram_imag):
    order_size = gram_real.shape[0]
    embedded = jnp.stack(
        [jnp.stack([gram_real, -gram_imag], axis=2), jnp.stack([gram_imag, gram_real], axis=2)],
        axis=1,
    ).reshape(2 * order_size, 2 * order_size)
    lower_factor = jnp.linalg.cholesky(embedded)
    identity = jnp.eye(2 * order_size, dtype=gram_real.dtype)
    inverse = jax.scipy.linalg.solve_triangular(lower_factor, identity, lower=True)
    blocks = inverse.reshape(order_size, 2, order_size, 2)
    return (blocks[:, 0, :, 0], blocks[:, 1, :, 0])


def right_block(inverse_real, inverse_imag):
    upper_half = jnp.concatenate([inverse_real.T, -inverse_imag.T], axis=1)
    lower_half = jnp.concatenate([inverse_imag.T, inverse_real.T], axis=1)
    return jnp.concatenate([upper_half, lower_half], axis=0)


def split_gram(matrix, vector_count):
    return (
        matrix[:vector_count, :vector_count] + matrix[vector_count:, vector_count:],
        matrix[:vector_count, vector_count:] - matrix[vector_count:, :vector_count],
    )


def combine_parts(part_real, part_imag, vector_count):
    return jnp.concatenate(
        [
            part_real[:, :vector_count] - part_imag[:, vector_count:],
            part_real[:, vector_count:] + part_imag[:, :vector_count],
        ],
        axis=1,
    )


def chebyshev(vectors, apply_matrix, lower_value, upper_value, first_image):
    centre = 0.5 * (upper_value + lower_value)
    spread = 0.5 * (upper_value - lower_value)
    previous = vectors
    first_image = apply_matrix(vectors)
    current = (first_image - centre * vectors) / spread
    following = 2.0 * (apply_matrix(current) - centre * current) / spread - previous
    previous, current = (current, following)
    return current


def on_device(force_constants, offsets, qpoints, lower_bound, upper_bound, start_vectors):
    cell_count, row_count, col_count = force_constants.shape
    qcount = qpoints.shape[0]
    vector_count = start_vectors.shape[1] // 2
    coefficients = phase_table(qpoints, offsets).reshape(2 * qcount, cell_count)
    partial_value = product(
        coefficients, force_constants.reshape(cell_count, row_count * col_count)
    )
    partial_value = partial_value.reshape(qcount, 2, row_count, col_count)
    owned_block = lax.all_to_all(partial_value, "pb", split_axis=0, concat_axis=3, tiled=True)
    dyn_real = owned_block[0, 0]
    dyn_imag = owned_block[0, 1]

    def accumulate(piece):
        return combine_parts(product(dyn_real, piece), product(dyn_imag, piece), vector_count)

    def apply_matrix(vectors):
        return accumulate(lax.all_gather(vectors, "row", axis=0, tiled=True))

    lower_value = lower_bound[0]
    upper_value = upper_bound[0]
    first_pass = chebyshev(start_vectors, apply_matrix, lower_value, upper_value, None)
    final_pass = chebyshev(first_pass, apply_matrix, lower_value, upper_value, None)
    image = apply_matrix(final_pass)
    over_total, proj_total = lax.psum(
        (inner_product(final_pass, final_pass), inner_product(final_pass, image)), "row"
    )
    over_real, over_imag = split_gram(over_total, vector_count)
    proj_real, proj_imag = split_gram(proj_total, vector_count)
    inverse_real, inverse_imag = factor_inverse(over_real, over_imag)
    basis_local = math.sqrt(MODES) * product(final_pass, right_block(inverse_real, inverse_imag))
    temp_real, temp_imag = complex_times(proj_real, proj_imag, inverse_real.T, -inverse_imag.T)
    ritz_real, ritz_imag = complex_times(inverse_real, inverse_imag, temp_real, temp_imag)
    ritz_local = jnp.concatenate([ritz_real, ritz_imag], axis=1)
    return (basis_local[None], ritz_local[None])


STEPS = 5
MESH = pl.DeviceIdType.MESH


def assemble_kernel(coef_ref, force_ref, high_ref, low_ref):
    cells, tile_rows, cols = force_ref.shape
    pairs = (cells - 1) // 2
    points = high_ref.shape[0]
    width = 256
    for at in range(cols // width):
        span = slice(at * width, (at + 1) * width)
        home = force_ref[0, :, span]
        real = [coef_ref[2 * q, 0] * home for q in range(points)]
        imag = [coef_ref[2 * q + 1, 0] * home for q in range(points)]
        for c in range(1, pairs + 1):
            first = force_ref[c, :, span]
            second = force_ref[c + pairs, :, span]
            total, difference = first + second, first - second
            for q in range(points):
                real[q] = real[q] + coef_ref[2 * q, c] * total
                imag[q] = imag[q] + coef_ref[2 * q + 1, c] * difference
        for q in range(points):
            for part, value in ((0, real[q]), (1, imag[q])):
                high = value.astype(jnp.bfloat16)
                high_ref[q, part, :, span] = high
                low_ref[q, part, :, span] = (value - high.astype(jnp.float32)).astype(jnp.bfloat16)


def assemble(coefficients, force_constants, points):
    cells, rows, cols = force_constants.shape
    tile = 16
    shape = jax.ShapeDtypeStruct((points, 2, rows, cols), jnp.bfloat16)
    block = pl.BlockSpec((points, 2, tile, cols), lambda i: (0, 0, i, 0))
    return pl.pallas_call(
        assemble_kernel,
        grid=(rows // tile,),
        out_shape=(shape, shape),
        in_specs=[
            pl.BlockSpec(memory_space=pltpu.SMEM),
            pl.BlockSpec((cells, tile, cols), lambda i: (0, i, 0)),
        ],
        out_specs=(block, block),
    )(coefficients, force_constants)


def sign_row(first, second):
    lane = lax.broadcasted_iota(jnp.int32, (1, 128), 1)
    return jnp.where(lane < 64, first, second).astype(jnp.float32)


def filter_kernel(
    bounds_ref, start_ref, high_ref, low_ref, final_ref, gram_ref,
    full, part, other, split, partner_bounds, sums, arrived,
    send_sem, recv_sem, x_send, x_recv, b_sem, g_send, g_recv,
):
    p = lax.axis_index("pb")
    row = lax.axis_index("row")
    rows = start_ref.shape[0]
    z, y, c = row // 4, (row // 2) % 2, row % 2
    position = z + p * (3 - 2 * z)
    owner = position < 2
    not_owner = position >= 2
    to_x = (1 - p, row)
    to_c = (p, row + 1 - 2 * c)
    to_y = (p, row + 2 - 4 * y)
    to_a = (p, row + 4 - 8 * (z % 2))
    to_b = (p, (3 - z) * 4 + y * 2 + c)
    near, far = 1 - p, p
    is_zero = jnp.where(position == 0, 1, 0)
    first = near + is_zero * (far - near)
    second = 1 - first
    mine = (z % 2) * 4 + y * 2 + c

    barrier = pltpu.get_barrier_semaphore()
    for target in (to_x, to_c, to_y, to_a, to_b):
        pl.semaphore_signal(barrier, inc=1, device_id=target, device_id_type=MESH)
    pl.semaphore_wait(barrier, 5)

    bound_copy = pltpu.make_async_remote_copy(
        src_ref=bounds_ref, dst_ref=partner_bounds, send_sem=b_sem.at[0], recv_sem=b_sem.at[1],
        device_id=to_x, device_id_type=MESH,
    )
    bound_copy.start()

    def block_rows(index):
        return pl.ds(pl.multiple_of(index * rows, 8), rows)

    @pl.when(owner)
    def _():
        full[0, 0, block_rows(mine), :] = start_ref[...]
        full[0, 1, block_rows(mine), :] = start_ref[...]

    bound_copy.wait()

    def send(slot, q, index, lane, target):
        view = full.at[slot, q, block_rows(index)]
        return pltpu.make_async_remote_copy(
            src_ref=view, dst_ref=view, send_sem=send_sem.at[q, lane],
            recv_sem=recv_sem.at[slot, q, index], device_id=target, device_id_type=MESH,
        )

    def lane_block(level, flipped_y, flipped_c):
        yy = 1 - y if flipped_y else y
        cc = 1 - c if flipped_c else c
        return level * 4 + yy * 2 + cc

    def head_sends(slot, q):
        index = lane_block(first, False, False)
        return (
            (position == 1, send(slot, q, index, 1, to_b)),
            (position <= 2, send(slot, q, index, 0, to_a)),
            (None, send(slot, q, index, 2, to_y)),
            (None, send(slot, q, index, 3, to_c)),
        )

    def tail_sends(slot, q):
        index = lane_block(second, False, False)
        return (
            (position == 1, send(slot, q, index, 5, to_b)),
            (position == 2, send(slot, q, index, 4, to_a)),
            (None, send(slot, q, index, 6, to_y)),
            (None, send(slot, q, index, 7, to_c)),
        )

    def across_sends(slot, q):
        return (
            send(slot, q, lane_block(first, True, False), 8, to_c),
            send(slot, q, lane_block(second, True, False), 9, to_c),
        )

    def guarded(condition, action):
        if condition is None:
            action()
        else:
            pl.when(condition)(action)

    def await_block(slot, q, index):
        send(slot, q, index, 0, to_c).wait_recv()

    def head(slot, q):
        pl.when(not_owner)(lambda: await_block(slot, q, lane_block(first, False, False)))
        for condition, copy in head_sends(slot, q):
            guarded(condition, copy.start)

    def tail(slot, q):
        await_block(slot, q, lane_block(second, False, False))
        for condition, copy in tail_sends(slot, q):
            guarded(condition, copy.start)

    def across(slot, q, which):
        await_block(slot, q, lane_block((first, second)[which], True, False))
        across_sends(slot, q)[which].start()

    def collect(slot, q):
        for flipped in (False, True):
            for level in (first, second):
                await_block(slot, q, lane_block(level, flipped, True))

    def await_sends(slot, q):
        for condition, copy in head_sends(slot, q) + tail_sends(slot, q):
            guarded(condition, copy.wait_send)
        for copy in across_sends(slot, q):
            copy.wait_send()

    def partial_copy(slot, q):
        return pltpu.make_async_remote_copy(
            src_ref=part.at[q], dst_ref=other.at[slot, q], send_sem=x_send.at[q],
            recv_sem=x_recv.at[slot, q], device_id=to_x, device_id_type=MESH,
        )

    def final_copy(slot, q):
        return pltpu.make_async_remote_copy(
            src_ref=full.at[slot, q, block_rows(mine)], dst_ref=other.at[slot, q],
            send_sem=x_send.at[q], recv_sem=x_recv.at[slot, q],
            device_id=to_x, device_id_type=MESH,
        )

    def multiply(slot, q, source):
        values = full[slot, source]
        upper = values.astype(jnp.bfloat16)
        split[:, :128] = upper
        split[:, 128:] = (values - upper.astype(jnp.float32)).astype(jnp.bfloat16)
        def image(which):
            wide = jnp.dot(high_ref[q, which], split[...], preferred_element_type=jnp.float32)
            rest = jnp.dot(low_ref[q, which], split[:, :128], preferred_element_type=jnp.float32)
            return wide[:, :128] + (wide[:, 128:] + rest)
        part[q] = image(0) + sign_row(-1.0, 1.0) * pltpu.roll(image(1), 64, 1)

    def update(slot, q, weight, keep):
        own = jnp.where(p == q, 1.0, 0.0)
        centre = own * bounds_ref[0:1, :] + (1.0 - own) * partner_bounds[0:1, :]
        spread = own * bounds_ref[1:2, :] + (1.0 - own) * partner_bounds[1:2, :]
        current = full[slot, q, block_rows(mine), :]
        previous = full[1 - slot, q, block_rows(mine), :]
        image = part[q] + other[slot, q]
        full[1 - slot, q, block_rows(mine), :] = (
            weight * (image - centre * current) / spread - jnp.where(keep, previous, 0.0)
        )

    def step(k, carry):
        slot = k % 2
        later = k > 0
        last = k == STEPS - 1
        middle = k < STEPS - 1
        head(slot, 0)
        pl.when(later)(lambda: head(slot, 1))

        @pl.when(jnp.logical_and(last, owner))
        def _():
            final_copy(slot, 0).start()
            final_copy(slot, 1).start()

        tail(slot, 0)
        pl.when(later)(lambda: tail(slot, 1))
        for which in (0, 1):
            across(slot, 0, which)
            pl.when(later)(functools.partial(across, slot, 1, which))
        collect(slot, 0)
        multiply(slot, 0, 0)
        pl.when(jnp.logical_and(middle, not_owner))(lambda: partial_copy(slot, 0).start())
        pl.when(later)(lambda: collect(slot, 1))
        multiply(slot, 1, jnp.where(later, 1, 0))
        await_sends(slot, 0)
        pl.when(later)(lambda: await_sends(slot, 1))
        pl.when(jnp.logical_and(middle, not_owner))(lambda: partial_copy(slot, 1).start())
        odd = slot == 0
        weight = jnp.where(odd, 1.0, 2.0)

        @pl.when(jnp.logical_and(middle, owner))
        def _():
            for q in (0, 1):
                partial_copy(slot, q).wait_recv()

                @pl.when(k == 0)
                def _():
                    full[1, q, block_rows(mine), :] = jnp.zeros((rows, 128), jnp.float32)

                update(slot, q, weight, slot == 1)

        @pl.when(jnp.logical_and(middle, not_owner))
        def _():
            partial_copy(slot, 0).wait_send()
            partial_copy(slot, 1).wait_send()

        return carry

    lax.fori_loop(0, STEPS, step, 0)
    slot = (STEPS - 1) % 2

    @pl.when(owner)
    def _():
        for q in (0, 1):
            final_copy(slot, q).wait_send()
            other[slot, q] = full[slot, q, block_rows(mine), :]

    @pl.when(not_owner)
    def _():
        final_copy(slot, 0).wait_recv()
        final_copy(slot, 1).wait_recv()

    final_ref[...] = other[slot, p]

    def gram(left, right):
        whole = lax.dot_general(
            left, right, (((0,), (0,)), ((), ())), precision=highest,
            preferred_element_type=jnp.float32,
        )
        return whole[:64] + sign_row(1.0, -1.0) * pltpu.roll(whole[64:], 64, 1)

    sums[5, 0] = gram(other[slot, 1 - p], part[1 - p])
    cross = pltpu.make_async_remote_copy(
        src_ref=sums.at[5, 0], dst_ref=arrived.at[4, 0], send_sem=g_send.at[4],
        recv_sem=g_recv.at[4], device_id=to_x, device_id_type=MESH,
    )
    cross.start()
    sums[0, 0] = gram(other[slot, p], other[slot, p])
    own_projected = gram(other[slot, p], part[p])
    cross.wait()
    sums[0, 1] = own_projected + arrived[4, 0]
    for stage, target in enumerate((to_c, to_y, to_a, to_b)):
        copy = pltpu.make_async_remote_copy(
            src_ref=sums.at[stage], dst_ref=arrived.at[stage], send_sem=g_send.at[stage],
            recv_sem=g_recv.at[stage], device_id=target, device_id_type=MESH,
        )
        copy.start()
        copy.wait()
        sums[stage + 1] = sums[stage] + arrived[stage]
    gram_ref[...] = sums[4]


def filtered(bounds, start_vectors, high, low):
    rows = start_vectors.shape[0]
    points, _, _, cols = high.shape
    vmem = pl.BlockSpec(memory_space=pltpu.VMEM)
    dma = pltpu.SemaphoreType.DMA
    return pl.pallas_call(
        filter_kernel,
        out_shape=(
            jax.ShapeDtypeStruct((rows, 128), jnp.float32),
            jax.ShapeDtypeStruct((2, 64, 128), jnp.float32),
        ),
        in_specs=[vmem] * 4,
        out_specs=(vmem, vmem),
        scratch_shapes=[
            pltpu.VMEM((2, points, cols, 128), jnp.float32),
            pltpu.VMEM((points, rows, 128), jnp.float32),
            pltpu.VMEM((2, points, rows, 128), jnp.float32),
            pltpu.VMEM((cols, 256), jnp.bfloat16),
            pltpu.VMEM((8, 128), jnp.float32),
            pltpu.VMEM((6, 2, 64, 128), jnp.float32),
            pltpu.VMEM((5, 2, 64, 128), jnp.float32),
            dma((points, 10)),
            dma((2, points, 8)),
            dma((points,)),
            dma((2, points)),
            dma((2,)),
            dma((5,)),
            dma((5,)),
        ],
        compiler_params=pltpu.CompilerParams(
            collective_id=0, has_side_effects=True, vmem_limit_bytes=56 * 1024 * 1024
        ),
    )(bounds, start_vectors, high, low)


def on_block(force_constants, offsets, qpoints, lower_bound, upper_bound, start_vectors):
    cell_count = force_constants.shape[0]
    qcount = qpoints.shape[0]
    vector_count = start_vectors.shape[1] // 2
    coefficients = phase_table(qpoints, offsets).reshape(2 * qcount, cell_count)
    high, low = assemble(coefficients, force_constants, qcount)
    centre = 0.5 * (upper_bound + lower_bound)
    spread = 0.5 * (upper_bound - lower_bound)
    bounds = jnp.broadcast_to(
        jnp.concatenate([centre, spread, jnp.zeros((6,), jnp.float32)])[:, None], (8, 128)
    )
    final_pass, grams = filtered(bounds, start_vectors, high, low)
    over_real, over_imag = grams[0, :, :vector_count], grams[0, :, vector_count:]
    proj_real, proj_imag = grams[1, :, :vector_count], grams[1, :, vector_count:]
    inverse_real, inverse_imag = factor_inverse(over_real, over_imag)
    basis_local = math.sqrt(MODES) * product(final_pass, right_block(inverse_real, inverse_imag))
    temp_real, temp_imag = complex_times(proj_real, proj_imag, inverse_real.T, -inverse_imag.T)
    ritz_real, ritz_imag = complex_times(inverse_real, inverse_imag, temp_real, temp_imag)
    ritz_local = jnp.concatenate([ritz_real, ritz_imag], axis=1)
    return (basis_local[None], ritz_local[None])


def solution(mesh):
    paired = mesh.shape["pb"] == 2 and mesh.shape["row"] == 16
    return jax.shard_map(
        on_block if paired else on_device,
        mesh=mesh,
        in_specs=(P(None, "row", "pb"), P(), P(), P("pb"), P("pb"), P("row", None)),
        out_specs=(P("pb", "row", None), P("pb", None, None)),
        check_vma=False,
    )
```

```python
import functools
import math

import jax
import jax.numpy as jnp
from jax import lax
from jax.experimental import pallas as pl
from jax.experimental.pallas import tpu as pltpu
from jax.sharding import PartitionSpec as P

MODES = 4608
QDEN = 8


highest = lax.Precision.HIGHEST


def product(left, right):
    return jnp.dot(left, right, precision=highest, preferred_element_type=jnp.float32)


def inner_product(left, right):
    return lax.dot_general(
        left, right, (((0,), (0,)), ((), ())), precision=highest, preferred_element_type=jnp.float32
    )


def complex_times(left_real, left_imag, right_real, right_imag):
    return (
        product(left_real, right_real) - product(left_imag, right_imag),
        product(left_real, right_imag) + product(left_imag, right_real),
    )


def phase_table(qpoints, offsets):
    turns = jnp.sum(qpoints[:, None, :] * offsets[None, :, :], axis=2)
    turns = jnp.mod(turns, QDEN)
    angle = 2.0 * math.pi / QDEN * turns.astype(jnp.float32)
    return jnp.stack([jnp.cos(angle), jnp.sin(angle)], axis=1)


def factor_inverse(gram_real, gram_imag):
    order_size = gram_real.shape[0]
    embedded = jnp.stack(
        [jnp.stack([gram_real, -gram_imag], axis=2), jnp.stack([gram_imag, gram_real], axis=2)],
        axis=1,
    ).reshape(2 * order_size, 2 * order_size)
    lower_factor = jnp.linalg.cholesky(embedded)
    identity = jnp.eye(2 * order_size, dtype=gram_real.dtype)
    inverse = jax.scipy.linalg.solve_triangular(lower_factor, identity, lower=True)
    blocks = inverse.reshape(order_size, 2, order_size, 2)
    return (blocks[:, 0, :, 0], blocks[:, 1, :, 0])


def right_block(inverse_real, inverse_imag):
    upper_half = jnp.concatenate([inverse_real.T, -inverse_imag.T], axis=1)
    lower_half = jnp.concatenate([inverse_imag.T, inverse_real.T], axis=1)
    return jnp.concatenate([upper_half, lower_half], axis=0)


def split_gram(matrix, vector_count):
    return (
        matrix[:vector_count, :vector_count] + matrix[vector_count:, vector_count:],
        matrix[:vector_count, vector_count:] - matrix[vector_count:, :vector_count],
    )


def combine_parts(part_real, part_imag, vector_count):
    return jnp.concatenate(
        [
            part_real[:, :vector_count] - part_imag[:, vector_count:],
            part_real[:, vector_count:] + part_imag[:, :vector_count],
        ],
        axis=1,
    )


def chebyshev(vectors, apply_matrix, lower_value, upper_value, first_image):
    centre = 0.5 * (upper_value + lower_value)
    spread = 0.5 * (upper_value - lower_value)
    previous = vectors
    first_image = apply_matrix(vectors)
    current = (first_image - centre * vectors) / spread
    following = 2.0 * (apply_matrix(current) - centre * current) / spread - previous
    previous, current = (current, following)
    return current


def on_device(force_constants, offsets, qpoints, lower_bound, upper_bound, start_vectors):
    cell_count, row_count, col_count = force_constants.shape
    qcount = qpoints.shape[0]
    vector_count = start_vectors.shape[1] // 2
    coefficients = phase_table(qpoints, offsets).reshape(2 * qcount, cell_count)
    partial_value = product(
        coefficients, force_constants.reshape(cell_count, row_count * col_count)
    )
    partial_value = partial_value.reshape(qcount, 2, row_count, col_count)
    owned_block = lax.all_to_all(partial_value, "pb", split_axis=0, concat_axis=3, tiled=True)
    dyn_real = owned_block[0, 0]
    dyn_imag = owned_block[0, 1]

    def accumulate(piece):
        return combine_parts(product(dyn_real, piece), product(dyn_imag, piece), vector_count)

    def apply_matrix(vectors):
        return accumulate(lax.all_gather(vectors, "row", axis=0, tiled=True))

    lower_value = lower_bound[0]
    upper_value = upper_bound[0]
    first_pass = chebyshev(start_vectors, apply_matrix, lower_value, upper_value, None)
    final_pass = chebyshev(first_pass, apply_matrix, lower_value, upper_value, None)
    image = apply_matrix(final_pass)
    over_total, proj_total = lax.psum(
        (inner_product(final_pass, final_pass), inner_product(final_pass, image)), "row"
    )
    over_real, over_imag = split_gram(over_total, vector_count)
    proj_real, proj_imag = split_gram(proj_total, vector_count)
    inverse_real, inverse_imag = factor_inverse(over_real, over_imag)
    basis_local = math.sqrt(MODES) * product(final_pass, right_block(inverse_real, inverse_imag))
    temp_real, temp_imag = complex_times(proj_real, proj_imag, inverse_real.T, -inverse_imag.T)
    ritz_real, ritz_imag = complex_times(inverse_real, inverse_imag, temp_real, temp_imag)
    ritz_local = jnp.concatenate([ritz_real, ritz_imag], axis=1)
    return (basis_local[None], ritz_local[None])


STEPS = 5
MESH = pl.DeviceIdType.MESH


def assemble_kernel(coef_ref, force_ref, high_ref, low_ref):
    cells, tile_rows, cols = force_ref.shape
    pairs = (cells - 1) // 2
    points = high_ref.shape[0]
    width = 256
    for at in range(cols // width):
        span = slice(at * width, (at + 1) * width)
        home = force_ref[0, :, span]
        real = [coef_ref[2 * q, 0] * home for q in range(points)]
        imag = [coef_ref[2 * q + 1, 0] * home for q in range(points)]
        for c in range(1, pairs + 1):
            first = force_ref[c, :, span]
            second = force_ref[c + pairs, :, span]
            total, difference = first + second, first - second
            for q in range(points):
                real[q] = real[q] + coef_ref[2 * q, c] * total
                imag[q] = imag[q] + coef_ref[2 * q + 1, c] * difference
        for q in range(points):
            for part, value in ((0, real[q]), (1, imag[q])):
                high = value.astype(jnp.bfloat16)
                high_ref[q, part, :, span] = high
                low_ref[q, part, :, span] = (value - high.astype(jnp.float32)).astype(jnp.bfloat16)


def assemble(coefficients, force_constants, points):
    cells, rows, cols = force_constants.shape
    tile = 48
    shape = jax.ShapeDtypeStruct((points, 2, rows, cols), jnp.bfloat16)
    block = pl.BlockSpec((points, 2, tile, cols), lambda i: (0, 0, i, 0))
    return pl.pallas_call(
        assemble_kernel,
        grid=(rows // tile,),
        out_shape=(shape, shape),
        in_specs=[
            pl.BlockSpec(memory_space=pltpu.SMEM),
            pl.BlockSpec((cells, tile, cols), lambda i: (0, i, 0)),
        ],
        out_specs=(block, block),
    )(coefficients, force_constants)


def sign_row(first, second):
    lane = lax.broadcasted_iota(jnp.int32, (1, 128), 1)
    return jnp.where(lane < 64, first, second).astype(jnp.float32)


def filter_kernel(
    bounds_ref, start_ref, high_ref, low_ref, final_ref, gram_ref,
    full, part, other, split, partner_bounds, sums, arrived,
    send_sem, recv_sem, x_send, x_recv, b_sem, g_send, g_recv,
):
    p = lax.axis_index("pb")
    row = lax.axis_index("row")
    rows = start_ref.shape[0]
    z, y, c = row // 4, (row // 2) % 2, row % 2
    position = z + p * (3 - 2 * z)
    owner = position < 2
    not_owner = position >= 2
    to_x = (1 - p, row)
    to_c = (p, row + 1 - 2 * c)
    to_y = (p, row + 2 - 4 * y)
    to_a = (p, row + 4 - 8 * (z % 2))
    to_b = (p, (3 - z) * 4 + y * 2 + c)
    near, far = 1 - p, p
    is_zero = jnp.where(position == 0, 1, 0)
    first = near + is_zero * (far - near)
    second = 1 - first
    mine = (z % 2) * 4 + y * 2 + c

    barrier = pltpu.get_barrier_semaphore()
    for target in (to_x, to_c, to_y, to_a, to_b):
        pl.semaphore_signal(barrier, inc=1, device_id=target, device_id_type=MESH)
    pl.semaphore_wait(barrier, 5)

    bound_copy = pltpu.make_async_remote_copy(
        src_ref=bounds_ref, dst_ref=partner_bounds, send_sem=b_sem.at[0], recv_sem=b_sem.at[1],
        device_id=to_x, device_id_type=MESH,
    )
    bound_copy.start()

    def block_rows(index):
        return pl.ds(pl.multiple_of(index * rows, 8), rows)

    @pl.when(owner)
    def _():
        full[0, 0, block_rows(mine), :] = start_ref[...]
        full[0, 1, block_rows(mine), :] = start_ref[...]

    bound_copy.wait()

    def send(slot, q, index, lane, target):
        view = full.at[slot, q, block_rows(index)]
        return pltpu.make_async_remote_copy(
            src_ref=view, dst_ref=view, send_sem=send_sem.at[q, lane],
            recv_sem=recv_sem.at[slot, q, index], device_id=target, device_id_type=MESH,
        )

    def lane_block(level, flipped_y, flipped_c):
        yy = 1 - y if flipped_y else y
        cc = 1 - c if flipped_c else c
        return level * 4 + yy * 2 + cc

    def head_sends(slot, q):
        index = lane_block(first, False, False)
        return (
            (position == 1, send(slot, q, index, 1, to_b)),
            (position <= 2, send(slot, q, index, 0, to_a)),
            (None, send(slot, q, index, 2, to_y)),
            (None, send(slot, q, index, 3, to_c)),
        )

    def tail_sends(slot, q):
        index = lane_block(second, False, False)
        return (
            (position == 1, send(slot, q, index, 5, to_b)),
            (position == 2, send(slot, q, index, 4, to_a)),
            (None, send(slot, q, index, 6, to_y)),
            (None, send(slot, q, index, 7, to_c)),
        )

    def across_sends(slot, q):
        return (
            send(slot, q, lane_block(first, True, False), 8, to_c),
            send(slot, q, lane_block(second, True, False), 9, to_c),
        )

    def guarded(condition, action):
        if condition is None:
            action()
        else:
            pl.when(condition)(action)

    def await_block(slot, q, index):
        send(slot, q, index, 0, to_c).wait_recv()

    def head(slot, q):
        pl.when(not_owner)(lambda: await_block(slot, q, lane_block(first, False, False)))
        for condition, copy in head_sends(slot, q):
            guarded(condition, copy.start)

    def tail(slot, q):
        await_block(slot, q, lane_block(second, False, False))
        for condition, copy in tail_sends(slot, q):
            guarded(condition, copy.start)

    def across(slot, q, which):
        await_block(slot, q, lane_block((first, second)[which], True, False))
        across_sends(slot, q)[which].start()

    def collect(slot, q):
        for flipped in (False, True):
            for level in (first, second):
                await_block(slot, q, lane_block(level, flipped, True))

    def await_sends(slot, q):
        for condition, copy in head_sends(slot, q) + tail_sends(slot, q):
            guarded(condition, copy.wait_send)
        for copy in across_sends(slot, q):
            copy.wait_send()

    def partial_copy(slot, q):
        return pltpu.make_async_remote_copy(
            src_ref=part.at[q], dst_ref=other.at[slot, q], send_sem=x_send.at[q],
            recv_sem=x_recv.at[slot, q], device_id=to_x, device_id_type=MESH,
        )

    def final_copy(slot, q):
        return pltpu.make_async_remote_copy(
            src_ref=full.at[slot, q, block_rows(mine)], dst_ref=other.at[slot, q],
            send_sem=x_send.at[q], recv_sem=x_recv.at[slot, q],
            device_id=to_x, device_id_type=MESH,
        )

    def multiply(slot, q, source):
        values = full[slot, source]
        upper = values.astype(jnp.bfloat16)
        split[:, :128] = upper
        split[:, 128:] = (values - upper.astype(jnp.float32)).astype(jnp.bfloat16)
        def image(which):
            wide = jnp.dot(high_ref[q, which], split[...], preferred_element_type=jnp.float32)
            rest = jnp.dot(low_ref[q, which], split[:, :128], preferred_element_type=jnp.float32)
            return wide[:, :128] + (wide[:, 128:] + rest)
        part[q] = image(0) + sign_row(-1.0, 1.0) * pltpu.roll(image(1), 64, 1)

    def update(slot, q, weight, keep):
        own = jnp.where(p == q, 1.0, 0.0)
        centre = own * bounds_ref[0:1, :] + (1.0 - own) * partner_bounds[0:1, :]
        spread = own * bounds_ref[1:2, :] + (1.0 - own) * partner_bounds[1:2, :]
        current = full[slot, q, block_rows(mine), :]
        previous = full[1 - slot, q, block_rows(mine), :]
        image = part[q] + other[slot, q]
        full[1 - slot, q, block_rows(mine), :] = (
            weight * (image - centre * current) / spread - jnp.where(keep, previous, 0.0)
        )

    def step(k, carry):
        slot = k % 2
        later = k > 0
        last = k == STEPS - 1
        middle = k < STEPS - 1
        head(slot, 0)
        pl.when(later)(lambda: head(slot, 1))

        @pl.when(jnp.logical_and(last, owner))
        def _():
            final_copy(slot, 0).start()
            final_copy(slot, 1).start()

        tail(slot, 0)
        pl.when(later)(lambda: tail(slot, 1))
        for which in (0, 1):
            across(slot, 0, which)
            pl.when(later)(functools.partial(across, slot, 1, which))
        collect(slot, 0)
        multiply(slot, 0, 0)
        pl.when(jnp.logical_and(middle, not_owner))(lambda: partial_copy(slot, 0).start())
        pl.when(later)(lambda: collect(slot, 1))
        multiply(slot, 1, jnp.where(later, 1, 0))
        await_sends(slot, 0)
        pl.when(later)(lambda: await_sends(slot, 1))
        pl.when(jnp.logical_and(middle, not_owner))(lambda: partial_copy(slot, 1).start())
        odd = slot == 0
        weight = jnp.where(odd, 1.0, 2.0)

        @pl.when(jnp.logical_and(middle, owner))
        def _():
            for q in (0, 1):
                partial_copy(slot, q).wait_recv()

                @pl.when(k == 0)
                def _():
                    full[1, q, block_rows(mine), :] = jnp.zeros((rows, 128), jnp.float32)

                update(slot, q, weight, slot == 1)

        @pl.when(jnp.logical_and(middle, not_owner))
        def _():
            partial_copy(slot, 0).wait_send()
            partial_copy(slot, 1).wait_send()

        return carry

    lax.fori_loop(0, STEPS, step, 0)
    slot = (STEPS - 1) % 2

    @pl.when(owner)
    def _():
        for q in (0, 1):
            final_copy(slot, q).wait_send()
            other[slot, q] = full[slot, q, block_rows(mine), :]

    @pl.when(not_owner)
    def _():
        final_copy(slot, 0).wait_recv()
        final_copy(slot, 1).wait_recv()

    final_ref[...] = other[slot, p]

    def gram(left, right):
        whole = lax.dot_general(
            left, right, (((0,), (0,)), ((), ())), precision=highest,
            preferred_element_type=jnp.float32,
        )
        return whole[:64] + sign_row(1.0, -1.0) * pltpu.roll(whole[64:], 64, 1)

    sums[5, 0] = gram(other[slot, 1 - p], part[1 - p])
    cross = pltpu.make_async_remote_copy(
        src_ref=sums.at[5, 0], dst_ref=arrived.at[4, 0], send_sem=g_send.at[4],
        recv_sem=g_recv.at[4], device_id=to_x, device_id_type=MESH,
    )
    cross.start()
    sums[0, 0] = gram(other[slot, p], other[slot, p])
    own_projected = gram(other[slot, p], part[p])
    cross.wait()
    sums[0, 1] = own_projected + arrived[4, 0]
    for stage, target in enumerate((to_c, to_y, to_a, to_b)):
        copy = pltpu.make_async_remote_copy(
            src_ref=sums.at[stage], dst_ref=arrived.at[stage], send_sem=g_send.at[stage],
            recv_sem=g_recv.at[stage], device_id=target, device_id_type=MESH,
        )
        copy.start()
        copy.wait()
        sums[stage + 1] = sums[stage] + arrived[stage]
    gram_ref[...] = sums[4]


def filtered(bounds, start_vectors, high, low):
    rows = start_vectors.shape[0]
    points, _, _, cols = high.shape
    vmem = pl.BlockSpec(memory_space=pltpu.VMEM)
    dma = pltpu.SemaphoreType.DMA
    return pl.pallas_call(
        filter_kernel,
        out_shape=(
            jax.ShapeDtypeStruct((rows, 128), jnp.float32),
            jax.ShapeDtypeStruct((2, 64, 128), jnp.float32),
        ),
        in_specs=[vmem] * 4,
        out_specs=(vmem, vmem),
        scratch_shapes=[
            pltpu.VMEM((2, points, cols, 128), jnp.float32),
            pltpu.VMEM((points, rows, 128), jnp.float32),
            pltpu.VMEM((2, points, rows, 128), jnp.float32),
            pltpu.VMEM((cols, 256), jnp.bfloat16),
            pltpu.VMEM((8, 128), jnp.float32),
            pltpu.VMEM((6, 2, 64, 128), jnp.float32),
            pltpu.VMEM((5, 2, 64, 128), jnp.float32),
            dma((points, 10)),
            dma((2, points, 8)),
            dma((points,)),
            dma((2, points)),
            dma((2,)),
            dma((5,)),
            dma((5,)),
        ],
        compiler_params=pltpu.CompilerParams(
            collective_id=0, has_side_effects=True, vmem_limit_bytes=56 * 1024 * 1024
        ),
    )(bounds, start_vectors, high, low)


def finish_kernel(scale, final_ref, gram_ref, basis_ref, ritz_ref):
    size = gram_ref.shape[1]
    tile = 8
    gram = [gram_ref[0, t * tile:(t + 1) * tile, :] for t in range(size // tile)]
    lane = lax.broadcasted_iota(jnp.int32, (tile, 128), 1)
    line = lax.broadcasted_iota(jnp.int32, (tile, 128), 0)
    inverse = [jnp.where(lane == line + t * tile, 1.0, 0.0) for t in range(size // tile)]
    turn = sign_row(-1.0, 1.0)
    for j in range(size):
        home, at = j // tile, j % tile
        row = gram[home][at:at + 1, :]
        pivot = row[:, j:j + 1]
        row = row / pivot
        mate = inverse[home][at:at + 1, :] / pivot
        row_turned = turn * pltpu.roll(row, 64, 1)
        mate_turned = turn * pltpu.roll(mate, 64, 1)
        for t in range(home, size // tile):
            real = gram[t][:, j:j + 1]
            imag = gram[t][:, 64 + j:65 + j]
            if t == home:
                below = line[:, :1] > at
                real = jnp.where(below, real, 0.0)
                imag = jnp.where(below, imag, 0.0)
            gram[t] = gram[t] - (real * row + imag * row_turned)
            inverse[t] = inverse[t] - (real * mate + imag * mate_turned)
    scaled = []
    for t in range(size // tile):
        diagonal = jnp.sum(jnp.where(lane == line + t * tile, gram[t], 0.0), axis=1, keepdims=True)
        scaled.append(inverse[t] / jnp.sqrt(diagonal))
    whole = jnp.concatenate(scaled, axis=0)
    paired = jnp.concatenate([whole, turn * pltpu.roll(whole, 64, 1)], axis=0)

    def against(left):
        return lax.dot_general(
            left, paired, (((1,), (1,)), ((), ())), precision=highest,
            preferred_element_type=jnp.float32,
        )

    basis_ref[...] = scale * against(final_ref[...])
    half = against(gram_ref[1])
    ritz_ref[...] = product(whole, jnp.concatenate([half, turn * pltpu.roll(half, 64, 1)], axis=0))


def finish(final_pass, grams, modes):
    vmem = pl.BlockSpec(memory_space=pltpu.VMEM)
    return pl.pallas_call(
        functools.partial(finish_kernel, math.sqrt(modes)),
        out_shape=(
            jax.ShapeDtypeStruct(final_pass.shape, jnp.float32),
            jax.ShapeDtypeStruct(grams.shape[1:], jnp.float32),
        ),
        in_specs=[vmem] * 2,
        out_specs=(vmem, vmem),
    )(final_pass, grams)


def on_block(force_constants, offsets, qpoints, lower_bound, upper_bound, start_vectors):
    cell_count = force_constants.shape[0]
    qcount = qpoints.shape[0]
    coefficients = phase_table(qpoints, offsets).reshape(2 * qcount, cell_count)
    high, low = assemble(coefficients, force_constants, qcount)
    centre = 0.5 * (upper_bound + lower_bound)
    spread = 0.5 * (upper_bound - lower_bound)
    bounds = jnp.broadcast_to(
        jnp.concatenate([centre, spread, jnp.zeros((6,), jnp.float32)])[:, None], (8, 128)
    )
    final_pass, grams = filtered(bounds, start_vectors, high, low)
    basis_local, ritz_local = finish(final_pass, grams, MODES)
    return (basis_local[None], ritz_local[None])


def solution(mesh):
    paired = mesh.shape["pb"] == 2 and mesh.shape["row"] == 16
    return jax.shard_map(
        on_block if paired else on_device,
        mesh=mesh,
        in_specs=(P(None, "row", "pb"), P(), P(), P("pb"), P("pb"), P("row", None)),
        out_specs=(P("pb", "row", None), P("pb", None, None)),
        check_vma=False,
    )
```

```python
import functools
import math

import jax
import jax.numpy as jnp
from jax import lax
from jax.experimental import pallas as pl
from jax.experimental.pallas import tpu as pltpu
from jax.sharding import PartitionSpec as P

MODES = 4608
QDEN = 8


highest = lax.Precision.HIGHEST


def product(left, right):
    return jnp.dot(left, right, precision=highest, preferred_element_type=jnp.float32)


def inner_product(left, right):
    return lax.dot_general(
        left, right, (((0,), (0,)), ((), ())), precision=highest, preferred_element_type=jnp.float32
    )


def complex_times(left_real, left_imag, right_real, right_imag):
    return (
        product(left_real, right_real) - product(left_imag, right_imag),
        product(left_real, right_imag) + product(left_imag, right_real),
    )


def phase_table(qpoints, offsets):
    turns = jnp.sum(qpoints[:, None, :] * offsets[None, :, :], axis=2)
    turns = jnp.mod(turns, QDEN)
    angle = 2.0 * math.pi / QDEN * turns.astype(jnp.float32)
    return jnp.stack([jnp.cos(angle), jnp.sin(angle)], axis=1)


def factor_inverse(gram_real, gram_imag):
    order_size = gram_real.shape[0]
    embedded = jnp.stack(
        [jnp.stack([gram_real, -gram_imag], axis=2), jnp.stack([gram_imag, gram_real], axis=2)],
        axis=1,
    ).reshape(2 * order_size, 2 * order_size)
    lower_factor = jnp.linalg.cholesky(embedded)
    identity = jnp.eye(2 * order_size, dtype=gram_real.dtype)
    inverse = jax.scipy.linalg.solve_triangular(lower_factor, identity, lower=True)
    blocks = inverse.reshape(order_size, 2, order_size, 2)
    return (blocks[:, 0, :, 0], blocks[:, 1, :, 0])


def right_block(inverse_real, inverse_imag):
    upper_half = jnp.concatenate([inverse_real.T, -inverse_imag.T], axis=1)
    lower_half = jnp.concatenate([inverse_imag.T, inverse_real.T], axis=1)
    return jnp.concatenate([upper_half, lower_half], axis=0)


def split_gram(matrix, vector_count):
    return (
        matrix[:vector_count, :vector_count] + matrix[vector_count:, vector_count:],
        matrix[:vector_count, vector_count:] - matrix[vector_count:, :vector_count],
    )


def combine_parts(part_real, part_imag, vector_count):
    return jnp.concatenate(
        [
            part_real[:, :vector_count] - part_imag[:, vector_count:],
            part_real[:, vector_count:] + part_imag[:, :vector_count],
        ],
        axis=1,
    )


def chebyshev(vectors, apply_matrix, lower_value, upper_value, first_image):
    centre = 0.5 * (upper_value + lower_value)
    spread = 0.5 * (upper_value - lower_value)
    previous = vectors
    first_image = apply_matrix(vectors)
    current = (first_image - centre * vectors) / spread
    following = 2.0 * (apply_matrix(current) - centre * current) / spread - previous
    previous, current = (current, following)
    return current


def on_device(force_constants, offsets, qpoints, lower_bound, upper_bound, start_vectors):
    cell_count, row_count, col_count = force_constants.shape
    qcount = qpoints.shape[0]
    vector_count = start_vectors.shape[1] // 2
    coefficients = phase_table(qpoints, offsets).reshape(2 * qcount, cell_count)
    partial_value = product(
        coefficients, force_constants.reshape(cell_count, row_count * col_count)
    )
    partial_value = partial_value.reshape(qcount, 2, row_count, col_count)
    owned_block = lax.all_to_all(partial_value, "pb", split_axis=0, concat_axis=3, tiled=True)
    dyn_real = owned_block[0, 0]
    dyn_imag = owned_block[0, 1]

    def accumulate(piece):
        return combine_parts(product(dyn_real, piece), product(dyn_imag, piece), vector_count)

    def apply_matrix(vectors):
        return accumulate(lax.all_gather(vectors, "row", axis=0, tiled=True))

    lower_value = lower_bound[0]
    upper_value = upper_bound[0]
    first_pass = chebyshev(start_vectors, apply_matrix, lower_value, upper_value, None)
    final_pass = chebyshev(first_pass, apply_matrix, lower_value, upper_value, None)
    image = apply_matrix(final_pass)
    over_total, proj_total = lax.psum(
        (inner_product(final_pass, final_pass), inner_product(final_pass, image)), "row"
    )
    over_real, over_imag = split_gram(over_total, vector_count)
    proj_real, proj_imag = split_gram(proj_total, vector_count)
    inverse_real, inverse_imag = factor_inverse(over_real, over_imag)
    basis_local = math.sqrt(MODES) * product(final_pass, right_block(inverse_real, inverse_imag))
    temp_real, temp_imag = complex_times(proj_real, proj_imag, inverse_real.T, -inverse_imag.T)
    ritz_real, ritz_imag = complex_times(inverse_real, inverse_imag, temp_real, temp_imag)
    ritz_local = jnp.concatenate([ritz_real, ritz_imag], axis=1)
    return (basis_local[None], ritz_local[None])


STEPS = 5
PIECES = 2
MESH = pl.DeviceIdType.MESH


def assemble_kernel(coef_ref, force_ref, high_ref, low_ref):
    cells, tile_rows, cols = force_ref.shape
    pairs = (cells - 1) // 2
    points = high_ref.shape[0]
    width = 256
    for at in range(cols // width):
        span = slice(at * width, (at + 1) * width)
        home = force_ref[0, :, span]
        real = [coef_ref[2 * q, 0] * home for q in range(points)]
        imag = [coef_ref[2 * q + 1, 0] * home for q in range(points)]
        for c in range(1, pairs + 1):
            first = force_ref[c, :, span]
            second = force_ref[c + pairs, :, span]
            total, difference = first + second, first - second
            for q in range(points):
                real[q] = real[q] + coef_ref[2 * q, c] * total
                imag[q] = imag[q] + coef_ref[2 * q + 1, c] * difference
        for q in range(points):
            for part, value in ((0, real[q]), (1, imag[q])):
                high = value.astype(jnp.bfloat16)
                high_ref[q, part, :, span] = high
                low_ref[q, part, :, span] = (value - high.astype(jnp.float32)).astype(jnp.bfloat16)


def assemble(coefficients, force_constants, points):
    cells, rows, cols = force_constants.shape
    tile = 48
    shape = jax.ShapeDtypeStruct((points, 2, rows, cols), jnp.bfloat16)
    block = pl.BlockSpec((points, 2, tile, cols), lambda i: (0, 0, i, 0))
    return pl.pallas_call(
        assemble_kernel,
        grid=(rows // tile,),
        out_shape=(shape, shape),
        in_specs=[
            pl.BlockSpec(memory_space=pltpu.SMEM),
            pl.BlockSpec((cells, tile, cols), lambda i: (0, i, 0)),
        ],
        out_specs=(block, block),
    )(coefficients, force_constants)


def sign_row(first, second):
    lane = lax.broadcasted_iota(jnp.int32, (1, 128), 1)
    return jnp.where(lane < 64, first, second).astype(jnp.float32)


def filter_kernel(
    bounds_ref, start_ref, high_ref, low_ref, final_ref, gram_ref,
    full, part, other, split, partner_bounds, sums, arrived,
    send_sem, recv_sem, x_send, x_recv, b_sem, g_send, g_recv,
):
    p = lax.axis_index("pb")
    row = lax.axis_index("row")
    rows = start_ref.shape[0]
    z, y, c = row // 4, (row // 2) % 2, row % 2
    position = z + p * (3 - 2 * z)
    owner = position < 2
    not_owner = position >= 2
    to_x = (1 - p, row)
    to_c = (p, row + 1 - 2 * c)
    to_y = (p, row + 2 - 4 * y)
    to_a = (p, row + 4 - 8 * (z % 2))
    to_b = (p, (3 - z) * 4 + y * 2 + c)
    near, far = 1 - p, p
    is_zero = jnp.where(position == 0, 1, 0)
    first = near + is_zero * (far - near)
    second = 1 - first
    mine = (z % 2) * 4 + y * 2 + c

    barrier = pltpu.get_barrier_semaphore()
    for target in (to_x, to_c, to_y, to_a, to_b):
        pl.semaphore_signal(barrier, inc=1, device_id=target, device_id_type=MESH)
    pl.semaphore_wait(barrier, 5)

    bound_copy = pltpu.make_async_remote_copy(
        src_ref=bounds_ref, dst_ref=partner_bounds, send_sem=b_sem.at[0], recv_sem=b_sem.at[1],
        device_id=to_x, device_id_type=MESH,
    )
    bound_copy.start()

    def block_rows(index):
        return pl.ds(pl.multiple_of(index * rows, 8), rows)

    @pl.when(owner)
    def _():
        full[0, 0, block_rows(mine), :] = start_ref[...]
        full[0, 1, block_rows(mine), :] = start_ref[...]

    bound_copy.wait()

    depth = rows // PIECES

    def send(slot, q, index, piece, lane, target):
        where = pl.ds(pl.multiple_of(index * rows + piece * depth, 8), depth)
        view = full.at[slot, q, where]
        return pltpu.make_async_remote_copy(
            src_ref=view, dst_ref=view, send_sem=send_sem.at[q, lane, piece],
            recv_sem=recv_sem.at[slot, q, index, piece], device_id=target, device_id_type=MESH,
        )

    def lane_block(level, flipped_y, flipped_c):
        yy = 1 - y if flipped_y else y
        cc = 1 - c if flipped_c else c
        return level * 4 + yy * 2 + cc

    def head_sends(slot, q, piece):
        index = lane_block(first, False, False)
        return (
            (position == 1, send(slot, q, index, piece, 1, to_b)),
            (position <= 2, send(slot, q, index, piece, 0, to_a)),
            (None, send(slot, q, index, piece, 2, to_y)),
            (None, send(slot, q, index, piece, 3, to_c)),
        )

    def tail_sends(slot, q, piece):
        index = lane_block(second, False, False)
        return (
            (position == 1, send(slot, q, index, piece, 5, to_b)),
            (position == 2, send(slot, q, index, piece, 4, to_a)),
            (None, send(slot, q, index, piece, 6, to_y)),
            (None, send(slot, q, index, piece, 7, to_c)),
        )

    def across_send(slot, q, piece, which):
        index = lane_block((first, second)[which], True, False)
        return send(slot, q, index, piece, 8 + which, to_c)

    def guarded(condition, action):
        if condition is None:
            action()
        else:
            pl.when(condition)(action)

    def await_block(slot, q, index, piece):
        send(slot, q, index, piece, 0, to_c).wait_recv()

    def head(slot, q, relay):
        for piece in range(PIECES):
            if relay:
                await_block(slot, q, lane_block(first, False, False), piece)
            for condition, copy in head_sends(slot, q, piece):
                guarded(condition, copy.start)

    def tail(slot, q):
        for piece in range(PIECES):
            await_block(slot, q, lane_block(second, False, False), piece)
            for condition, copy in tail_sends(slot, q, piece):
                guarded(condition, copy.start)

    def across(slot, q):
        for which in (0, 1):
            for piece in range(PIECES):
                await_block(slot, q, lane_block((first, second)[which], True, False), piece)
                across_send(slot, q, piece, which).start()

    def collect(slot, q):
        for flipped in (False, True):
            for level in (first, second):
                for piece in range(PIECES):
                    await_block(slot, q, lane_block(level, flipped, True), piece)

    def gathered(slot, q):
        across(slot, q)
        collect(slot, q)

    def await_sends(slot, q):
        for piece in range(PIECES):
            for condition, copy in head_sends(slot, q, piece) + tail_sends(slot, q, piece):
                guarded(condition, copy.wait_send)
            for which in (0, 1):
                across_send(slot, q, piece, which).wait_send()

    def partial_copy(slot, q):
        return pltpu.make_async_remote_copy(
            src_ref=part.at[q], dst_ref=other.at[slot, q], send_sem=x_send.at[q],
            recv_sem=x_recv.at[slot, q], device_id=to_x, device_id_type=MESH,
        )

    def final_copy(slot, q):
        return pltpu.make_async_remote_copy(
            src_ref=full.at[slot, q, block_rows(mine)], dst_ref=other.at[slot, q],
            send_sem=x_send.at[q], recv_sem=x_recv.at[slot, q],
            device_id=to_x, device_id_type=MESH,
        )

    def divide(slot, q):
        values = full[slot, q]
        upper = values.astype(jnp.bfloat16)
        split[:, :128] = upper
        split[:, 128:] = (values - upper.astype(jnp.float32)).astype(jnp.bfloat16)

    def multiply(q):
        def image(which):
            wide = jnp.dot(high_ref[q, which], split[...], preferred_element_type=jnp.float32)
            rest = jnp.dot(low_ref[q, which], split[:, :128], preferred_element_type=jnp.float32)
            return wide[:, :128] + (wide[:, 128:] + rest)
        part[q] = image(0) + sign_row(-1.0, 1.0) * pltpu.roll(image(1), 64, 1)

    def update(slot, q, weight, keep):
        own = jnp.where(p == q, 1.0, 0.0)
        centre = own * bounds_ref[0:1, :] + (1.0 - own) * partner_bounds[0:1, :]
        spread = own * bounds_ref[1:2, :] + (1.0 - own) * partner_bounds[1:2, :]
        current = full[slot, q, block_rows(mine), :]
        previous = full[1 - slot, q, block_rows(mine), :]
        image = part[q] + other[slot, q]
        full[1 - slot, q, block_rows(mine), :] = (
            weight * (image - centre * current) / spread - jnp.where(keep, previous, 0.0)
        )

    def step(k, carry):
        slot = k % 2
        later = k > 0
        middle = k < STEPS - 1
        weight = jnp.where(slot == 0, 1.0, 2.0)
        for q in (0, 1):
            if q == 0:
                gathered(slot, q)
                divide(slot, q)
            else:
                @pl.when(later)
                def _():
                    gathered(slot, q)
                    divide(slot, q)

            @pl.when(jnp.logical_and(later, not_owner))
            def _():
                partial_copy(1 - slot, q).wait_send()

            multiply(q)
            guarded(None if q == 0 else later, functools.partial(await_sends, slot, q))
            pl.when(jnp.logical_and(middle, not_owner))(partial_copy(slot, q).start)

            other_slot, other_q, ready = (slot, 1, later) if q == 0 else (1 - slot, 0, middle)
            pl.when(jnp.logical_and(ready, not_owner))(
                functools.partial(head, other_slot, other_q, True)
            )
            pl.when(ready)(functools.partial(tail, other_slot, other_q))

            @pl.when(jnp.logical_and(middle, owner))
            def _():
                partial_copy(slot, q).wait_recv()

                @pl.when(k == 0)
                def _():
                    full[1, q, block_rows(mine), :] = jnp.zeros((rows, 128), jnp.float32)

                update(slot, q, weight, slot == 1)
                head(1 - slot, q, False)

                @pl.when(k == STEPS - 2)
                def _():
                    final_copy(1 - slot, q).start()

        return carry

    pl.when(owner)(functools.partial(head, 0, 0, False))
    pl.when(not_owner)(functools.partial(head, 0, 0, True))
    tail(0, 0)
    lax.fori_loop(0, STEPS, step, 0)
    slot = (STEPS - 1) % 2

    @pl.when(owner)
    def _():
        for q in (0, 1):
            final_copy(slot, q).wait_send()
            other[slot, q] = full[slot, q, block_rows(mine), :]

    @pl.when(not_owner)
    def _():
        final_copy(slot, 0).wait_recv()
        final_copy(slot, 1).wait_recv()

    final_ref[...] = other[slot, p]

    def gram(left, right):
        whole = lax.dot_general(
            left, right, (((0,), (0,)), ((), ())), precision=highest,
            preferred_element_type=jnp.float32,
        )
        return whole[:64] + sign_row(1.0, -1.0) * pltpu.roll(whole[64:], 64, 1)

    sums[5, 0] = gram(other[slot, 1 - p], part[1 - p])
    cross = pltpu.make_async_remote_copy(
        src_ref=sums.at[5, 0], dst_ref=arrived.at[4, 0], send_sem=g_send.at[4],
        recv_sem=g_recv.at[4], device_id=to_x, device_id_type=MESH,
    )
    cross.start()
    sums[0, 0] = gram(other[slot, p], other[slot, p])
    own_projected = gram(other[slot, p], part[p])
    cross.wait()
    sums[0, 1] = own_projected + arrived[4, 0]
    for stage, target in enumerate((to_c, to_y, to_a, to_b)):
        copy = pltpu.make_async_remote_copy(
            src_ref=sums.at[stage], dst_ref=arrived.at[stage], send_sem=g_send.at[stage],
            recv_sem=g_recv.at[stage], device_id=target, device_id_type=MESH,
        )
        copy.start()
        copy.wait()
        sums[stage + 1] = sums[stage] + arrived[stage]
    gram_ref[...] = sums[4]


def filtered(bounds, start_vectors, high, low):
    rows = start_vectors.shape[0]
    points, _, _, cols = high.shape
    vmem = pl.BlockSpec(memory_space=pltpu.VMEM)
    dma = pltpu.SemaphoreType.DMA
    return pl.pallas_call(
        filter_kernel,
        out_shape=(
            jax.ShapeDtypeStruct((rows, 128), jnp.float32),
            jax.ShapeDtypeStruct((2, 64, 128), jnp.float32),
        ),
        in_specs=[vmem] * 4,
        out_specs=(vmem, vmem),
        scratch_shapes=[
            pltpu.VMEM((2, points, cols, 128), jnp.float32),
            pltpu.VMEM((points, rows, 128), jnp.float32),
            pltpu.VMEM((2, points, rows, 128), jnp.float32),
            pltpu.VMEM((cols, 256), jnp.bfloat16),
            pltpu.VMEM((8, 128), jnp.float32),
            pltpu.VMEM((6, 2, 64, 128), jnp.float32),
            pltpu.VMEM((5, 2, 64, 128), jnp.float32),
            dma((points, 10, PIECES)),
            dma((2, points, 8, PIECES)),
            dma((points,)),
            dma((2, points)),
            dma((2,)),
            dma((5,)),
            dma((5,)),
        ],
        compiler_params=pltpu.CompilerParams(
            collective_id=0, has_side_effects=True, vmem_limit_bytes=56 * 1024 * 1024
        ),
    )(bounds, start_vectors, high, low)


def finish_kernel(scale, final_ref, gram_ref, basis_ref, ritz_ref):
    size = gram_ref.shape[1]
    tile = 8
    gram = [gram_ref[0, t * tile:(t + 1) * tile, :] for t in range(size // tile)]
    lane = lax.broadcasted_iota(jnp.int32, (tile, 128), 1)
    line = lax.broadcasted_iota(jnp.int32, (tile, 128), 0)
    inverse = [jnp.where(lane == line + t * tile, 1.0, 0.0) for t in range(size // tile)]
    turn = sign_row(-1.0, 1.0)
    for j in range(size):
        home, at = j // tile, j % tile
        row = gram[home][at:at + 1, :]
        pivot = row[:, j:j + 1]
        row = row / pivot
        mate = inverse[home][at:at + 1, :] / pivot
        row_turned = turn * pltpu.roll(row, 64, 1)
        mate_turned = turn * pltpu.roll(mate, 64, 1)
        for t in range(home, size // tile):
            real = gram[t][:, j:j + 1]
            imag = gram[t][:, 64 + j:65 + j]
            if t == home:
                below = line[:, :1] > at
                real = jnp.where(below, real, 0.0)
                imag = jnp.where(below, imag, 0.0)
            gram[t] = gram[t] - (real * row + imag * row_turned)
            inverse[t] = inverse[t] - (real * mate + imag * mate_turned)
    scaled = []
    for t in range(size // tile):
        diagonal = jnp.sum(jnp.where(lane == line + t * tile, gram[t], 0.0), axis=1, keepdims=True)
        scaled.append(inverse[t] / jnp.sqrt(diagonal))
    whole = jnp.concatenate(scaled, axis=0)
    paired = jnp.concatenate([whole, turn * pltpu.roll(whole, 64, 1)], axis=0)

    def against(left):
        return lax.dot_general(
            left, paired, (((1,), (1,)), ((), ())), precision=highest,
            preferred_element_type=jnp.float32,
        )

    basis_ref[...] = scale * against(final_ref[...])
    half = against(gram_ref[1])
    ritz_ref[...] = product(whole, jnp.concatenate([half, turn * pltpu.roll(half, 64, 1)], axis=0))


def finish(final_pass, grams, modes):
    vmem = pl.BlockSpec(memory_space=pltpu.VMEM)
    return pl.pallas_call(
        functools.partial(finish_kernel, math.sqrt(modes)),
        out_shape=(
            jax.ShapeDtypeStruct(final_pass.shape, jnp.float32),
            jax.ShapeDtypeStruct(grams.shape[1:], jnp.float32),
        ),
        in_specs=[vmem] * 2,
        out_specs=(vmem, vmem),
    )(final_pass, grams)


def on_block(force_constants, offsets, qpoints, lower_bound, upper_bound, start_vectors):
    cell_count = force_constants.shape[0]
    qcount = qpoints.shape[0]
    coefficients = phase_table(qpoints, offsets).reshape(2 * qcount, cell_count)
    high, low = assemble(coefficients, force_constants, qcount)
    centre = 0.5 * (upper_bound + lower_bound)
    spread = 0.5 * (upper_bound - lower_bound)
    bounds = jnp.broadcast_to(
        jnp.concatenate([centre, spread, jnp.zeros((6,), jnp.float32)])[:, None], (8, 128)
    )
    final_pass, grams = filtered(bounds, start_vectors, high, low)
    basis_local, ritz_local = finish(final_pass, grams, MODES)
    return (basis_local[None], ritz_local[None])


def solution(mesh):
    paired = mesh.shape["pb"] == 2 and mesh.shape["row"] == 16
    return jax.shard_map(
        on_block if paired else on_device,
        mesh=mesh,
        in_specs=(P(None, "row", "pb"), P(), P(), P("pb"), P("pb"), P("row", None)),
        out_specs=(P("pb", "row", None), P("pb", None, None)),
        check_vma=False,
    )
```
